32 devices in a mesh: grp: 2 (over y), head: 16 (over z, x, core).
Axes of the slice: x: 2, y: 2, z: 4, core: 2. Of those that a mesh axis runs over, the one named last changes fastest.
Arguments:
- queries: bfloat16 [32, 16, 576], P('grp', 'head'), parts along dimension 0, may hold values from -32 to 32
- kv_pages: bfloat16 [16384, 64, 576], P(('grp', 'head')), parts along dimension 0, may hold values from -8 to 8
- page_table: int32 [32, 512], P('grp'), parts along dimension 0, may hold values from 0 to 8191, as said below
- lengths: int32 [32], P('grp'), parts along dimension 0, may hold values from 2048 to 32768
- selected: int32 [32, 32], P('grp'), parts along dimension 0, may hold values from 0 to 511, as said below
Outputs:
- attended: bfloat16 [32, 16, 512], P('grp', 'head'), parts along dimension 0
The draws below stay inside these ranges and needn't reach their ends.
There are 2 independent parts, one for each index of `grp`. The reference program is written for one: setup_inputs(seed, part) draws one part's arguments, and reference() takes and returns one part's arrays. A program takes and returns all parts, laid end to end along the dimension named above; each array names one. Nothing has to cross between parts.
Inputs may be any that keep to these rules, and one draw needn't show every extreme that they name: `page_table`: every block of every request names a different page of the pool; the pages named by selected blocks fall at most 96 into one aligned run of 512 pages (one device's share of the pool), and some run holds exactly 96 of them. `selected`: each row names 32 different blocks of its request below ceil(lengths / 64); the first is the last such block.
All inputs are finite; a program needn't handle non-finite values.
Results may differ from the reference program's by a relative error of at most 0.0034.
Values may be sent and summed in bfloat16 or wider, within the bound.
No kernel may reach another device: no remote copies, remote signals or barrier semaphores. Data moves between devices by JAX's collectives and lax.ppermute only.
A program may use at most 128 MiB of HBM per device.

```python
import math
import jax
import jax.numpy as jnp
from jax import lax

LAT = 512
ROPE = 64
HEADS = 16
PAGE = 64
SEL = 32
CTX = 32768
REQS = 16
NBLK = 512
PAGES = 8192
PAGES_DEV = 512


def request_plan(key):
    base_key = jax.random.fold_in(key, 7)
    subkeys = jax.random.split(base_key, 7)
    lengths = jax.random.randint(subkeys[0], (REQS,), SEL * PAGE, CTX + 1).astype(jnp.int32)
    longest = jax.random.randint(subkeys[1], (), 0, REQS)
    shortest = (longest + 1 + jax.random.randint(subkeys[2], (), 0, REQS - 1)) % REQS
    lengths = lengths.at[longest].set(CTX).at[shortest].set(SEL * PAGE)
    blocks_live = (lengths + PAGE - 1) // PAGE
    column = jnp.arange(NBLK, dtype=jnp.int32)[None, :]
    noise_values = jax.random.randint(subkeys[3], (REQS, NBLK), 0, 65536)
    order_key = noise_values * NBLK + column + jnp.where(column >= blocks_live[:, None], 1 << 30, 0)
    order_key = jnp.where(column == blocks_live[:, None] - 1, -1, order_key)
    selected = jnp.argsort(order_key, axis=1)[:, :SEL].astype(jnp.int32)
    device_total = PAGES // PAGES_DEV
    pair_total = REQS * SEL
    mean_load = pair_total // device_total
    quarter = mean_load // 4
    bound_one = 3 * mean_load
    bound_two = bound_one + 2 * quarter
    bound_three = bound_one + 3 * quarter
    spread = jax.random.permutation(subkeys[4], pair_total)
    dev_order = jax.random.permutation(subkeys[5], device_total)
    slot_index = jnp.arange(pair_total, dtype=jnp.int32)
    within = slot_index % (4 * mean_load)
    group_index = slot_index // (4 * mean_load)
    rank_in = jnp.where(within < bound_one, 0, jnp.where(within < bound_two, 1, jnp.where(within < bound_three, 2, 3)))
    start_index = jnp.where(rank_in == 0, 0, jnp.where(rank_in == 1, bound_one, jnp.where(rank_in == 2, bound_two, bound_three)))
    device = dev_order[4 * group_index + rank_in]
    slot_page = (device * PAGES_DEV + within - start_index).astype(jnp.int32)
    pair_page = jnp.zeros((pair_total,), jnp.int32).at[spread].set(slot_page)
    rank_of = jnp.argsort(dev_order)
    load_kind = rank_of % 4
    used_count = jnp.where(load_kind == 0, 3 * mean_load, jnp.where(load_kind == 1, 2 * quarter, quarter))
    every_page = jnp.arange(PAGES, dtype=jnp.int32)
    free_mask = every_page % PAGES_DEV >= used_count[every_page // PAGES_DEV]
    shuffled = jax.random.permutation(subkeys[6], PAGES)
    free_order = shuffled[jnp.argsort(jnp.where(free_mask[shuffled], 0, 1))]
    flat_sel = (jnp.arange(REQS, dtype=jnp.int32)[:, None] * NBLK + selected).reshape(-1)
    chosen = jnp.zeros((PAGES,), jnp.int32).at[flat_sel].set(1)
    chosen_page = jnp.zeros((PAGES,), jnp.int32).at[flat_sel].set(pair_page)
    rest_rank = jnp.clip(jnp.cumsum(1 - chosen) - 1, 0, PAGES - 1)
    page_map = jnp.where(chosen == 1, chosen_page, free_order[rest_rank])
    return (lengths, selected, page_map.reshape(REQS, NBLK).astype(jnp.int32))


def cache_block(key, page):
    inner_key = jax.random.fold_in(jax.random.fold_in(key, 11), page)
    key_rows = jax.random.fold_in(inner_key, 0)
    row_values = jax.random.normal(key_rows, (PAGE, LAT + ROPE))
    return jnp.clip(row_values, -8.0, 8.0)


def draw_kv_pages(key, part):

    def one_page(page):
        return cache_block(key, page).astype(jnp.bfloat16)
    return lax.map(one_page, jnp.arange(PAGES, dtype=jnp.int32))


def draw_page_table(key, part):
    return request_plan(key)[2]


def draw_lengths(key, part):
    return request_plan(key)[0]


def draw_selected(key, part):
    return request_plan(key)[1]


def draw_queries(key, part):
    inner_key = jax.random.fold_in(key, 17)
    drawn = 0.7 * jax.random.normal(inner_key, (REQS, HEADS, LAT + ROPE))
    return jnp.clip(drawn, -32.0, 32.0).astype(jnp.bfloat16)


def setup_inputs(seed: int = 0, part: int = 0) -> dict:
    key_of = jax.random.split(jax.random.key(seed), 6)
    own_keys = jax.random.split(jax.random.fold_in(key_of[5], part), 6)
    queries = draw_queries(jax.random.fold_in(jax.random.fold_in(key_of[5], part), 71), part)
    kv_pages = draw_kv_pages(jax.random.fold_in(jax.random.fold_in(key_of[5], part), 71), part)
    page_table = draw_page_table(jax.random.fold_in(jax.random.fold_in(key_of[5], part), 71), part)
    lengths = draw_lengths(jax.random.fold_in(jax.random.fold_in(key_of[5], part), 71), part)
    selected = draw_selected(jax.random.fold_in(jax.random.fold_in(key_of[5], part), 71), part)
    return {"queries": queries, "kv_pages": kv_pages, "page_table": page_table, "lengths": lengths, "selected": selected}


SOFTMAX_SCALE = (0.1 * math.log(40.0) + 1.0) ** 2 / math.sqrt(192.0)

def reference(queries, kv_pages, page_table, lengths, selected):
    page_ids = jnp.take_along_axis(page_table, selected, axis=1)
    gathered = kv_pages[page_ids]
    positions = selected[:, :, None] * PAGE + jnp.arange(PAGE, dtype=jnp.int32)[None, None, :]
    live_mask = positions < lengths[:, None, None]
    scores = jnp.einsum('rhd,rstd->rhst', queries.astype(jnp.float32), gathered.astype(jnp.float32)) * SOFTMAX_SCALE
    masked = jnp.where(live_mask[:, None], scores, jnp.float32(-1e+30))
    row_top = lax.optimization_barrier(jnp.max(masked, axis=(2, 3), keepdims=True))
    weights = jnp.where(live_mask[:, None], jnp.exp(masked - row_top), jnp.float32(0.0))
    totals = lax.optimization_barrier(jnp.sum(weights, axis=(2, 3)))
    rounded = weights.astype(jnp.bfloat16)
    numer_sum = jnp.einsum('rhst,rste->rhe', rounded.astype(jnp.float32), gathered[..., :LAT].astype(jnp.float32))
    return (numer_sum / totals[..., None]).astype(jnp.bfloat16)
```

```python
import functools
import math

import jax
import jax.numpy as jnp
from jax import lax
from jax.experimental import pallas as pl
from jax.experimental.pallas import tpu as pltpu
from jax.sharding import PartitionSpec as P

ROPE = 64
LANES = 128
NEG = -1e30

SOFTMAX_SCALE = (0.1 * math.log(40.0) + 1.0) ** 2 / math.sqrt(192.0)


def attend_kernel(
    sizes, lengths_ref, table_ref, picks_ref, queries_ref, pool_ref, out_ref,
    pages, scores, tops, numer, sems,
):
    reqs, heads, latent, chunk = sizes
    tiles, tokens, channels, width = pages.shape
    picks, blocks = picks_ref.shape[0], table_ref.shape[1]
    pool = pool_ref.shape[2]
    chunks = tokens // chunk
    first_page = lax.axis_index("head") * pool

    block_lane = lax.broadcasted_iota(jnp.int32, (picks, blocks), 1)
    pool_lane = lax.broadcasted_iota(jnp.int32, (picks, pool), 1)
    owner_all = jnp.zeros((picks, pool), jnp.float32)
    count_all = jnp.zeros((picks, pool), jnp.float32)
    for r in range(reqs):
        pick = picks_ref[:, r : r + 1]
        row = table_ref[r : r + 1, :].astype(jnp.float32)
        page = jnp.sum(
            jnp.where(block_lane == pick, row, 0.0), axis=1, keepdims=True
        ).astype(jnp.int32)
        count = jnp.clip(lengths_ref[r] - pick * tokens, 0, tokens)
        hit = pool_lane == page - first_page
        owner_all = jnp.where(hit, float(r + 1), owner_all)
        count_all = jnp.where(hit, count.astype(jnp.float32), count_all)
    owner = jnp.sum(owner_all, axis=0, keepdims=True)
    count = jnp.sum(count_all, axis=0, keepdims=True).astype(jnp.int32)

    def lanes(x, tile):
        return x[:, tile * width : (tile + 1) * width]

    needed = [jnp.max(lanes(owner, tile)) > 0.5 for tile in range(tiles)]
    owner = owner.astype(jnp.int32) - 1

    def fetch(tile, part):
        return pltpu.make_async_copy(
            pool_ref.at[pl.ds(part * chunk, chunk), :, pl.ds(tile * width, width)],
            pages.at[tile, pl.ds(part * chunk, chunk)],
            sems.at[tile, part],
        )

    for tile in range(tiles):
        @pl.when(needed[tile])
        def _(tile=tile):
            for part in range(chunks):
                fetch(tile, part).start()

    tops[...] = jnp.full(tops.shape, NEG, jnp.float32)
    numer[...] = jnp.zeros(numer.shape, jnp.float32)
    group = 2 if width == LANES else 1

    for tile in range(tiles):
        @pl.when(needed[tile])
        def _(tile=tile):
            own = lanes(owner, tile)
            live = lanes(count, tile)
            own_wide = jnp.concatenate([own] * group, axis=1)

            @pl.loop(0, chunks)
            def _(part):
                fetch(tile, part).wait()
                top = tops[tile]
                for t in range(0, chunk, group):
                    token = part * chunk + t
                    keys = [pages[tile, token + g] for g in range(group)]
                    both = jnp.dot(
                        queries_ref[...],
                        jnp.concatenate(keys, axis=1),
                        preferred_element_type=jnp.float32,
                    )
                    mine = both[:heads]
                    for r in range(1, reqs):
                        mine = jnp.where(own_wide == r, both[r * heads : (r + 1) * heads], mine)
                    for g in range(group):
                        score = mine[:, g * width : (g + 1) * width] * SOFTMAX_SCALE
                        score = jnp.where(live > token + g, score, NEG)
                        scores[tile, token + g] = score
                        top = jnp.maximum(top, score)
                tops[tile] = top

    row_top = []
    for r in range(reqs):
        best = jnp.full((heads, width), NEG, jnp.float32)
        for tile in range(tiles):
            best = jnp.maximum(best, jnp.where(lanes(owner, tile) == r, tops[tile], NEG))
        row_top.append(jnp.max(best, axis=1, keepdims=True))

    total = [jnp.zeros((heads, width), jnp.float32) for _ in range(reqs)]
    sums = tops
    for tile in range(tiles):
        own = lanes(owner, tile)
        shift = jnp.zeros((heads, width), jnp.float32)
        for r in range(reqs):
            shift = jnp.where(own == r, row_top[r], shift)
        sums[tile] = jnp.zeros((heads, width), jnp.float32)

        @pl.when(needed[tile])
        def _(tile=tile, own=own, shift=shift):
            live = lanes(count, tile)

            @pl.loop(0, chunks)
            def _(part):
                acc = sums[tile]
                weights, values = [], []
                for t in range(chunk):
                    token = part * chunk + t
                    weight = jnp.where(live > token, jnp.exp(scores[tile, token] - shift), 0.0)
                    acc = acc + weight
                    spread = [jnp.where(own == r, weight, 0.0).astype(jnp.bfloat16) for r in range(reqs)]
                    weights.append(jnp.concatenate(spread, axis=0))
                    values.append(pages[tile, token, :latent])
                sums[tile] = acc
                numer[...] += lax.dot_general(
                    jnp.concatenate(weights, axis=1),
                    jnp.concatenate(values, axis=1),
                    (((1,), (1,)), ((), ())),
                    preferred_element_type=jnp.float32,
                )

    tail = lax.broadcasted_iota(jnp.int32, (heads, LANES), 1)
    for r in range(reqs):
        total = jnp.zeros((heads, width), jnp.float32)
        for tile in range(tiles):
            total = total + jnp.where(lanes(owner, tile) == r, sums[tile], 0.0)
        total = jnp.sum(total, axis=1, keepdims=True)
        out_ref[r, :, :latent] = numer[r * heads : (r + 1) * heads]
        out_ref[r, :, latent:] = jnp.where(tail == 0, row_top[r], jnp.where(tail == 1, total, 0.0))


def attend(queries, pool, page_table, lengths, selected):
    reqs, heads, channels = queries.shape
    tokens, _, pages_dev = pool.shape
    latent = channels - ROPE
    width = LANES if pages_dev % LANES == 0 else pages_dev
    tiles = pages_dev // width
    chunk = math.gcd(8, tokens)
    rows = reqs * heads
    vmem = pl.BlockSpec(memory_space=pltpu.VMEM)
    return pl.pallas_call(
        functools.partial(attend_kernel, (reqs, heads, latent, chunk)),
        out_shape=jax.ShapeDtypeStruct((reqs, heads, latent + LANES), jnp.float32),
        in_specs=[
            pl.BlockSpec(memory_space=pltpu.SMEM), vmem, vmem, vmem,
            pl.BlockSpec(memory_space=pl.ANY),
        ],
        out_specs=vmem,
        scratch_shapes=[
            pltpu.VMEM((tiles, tokens, channels, width), jnp.bfloat16),
            pltpu.VMEM((tiles, tokens, heads, width), jnp.float32),
            pltpu.VMEM((tiles, heads, width), jnp.float32),
            pltpu.VMEM((rows, latent), jnp.float32),
            pltpu.SemaphoreType.DMA((tiles, tokens // chunk)),
        ],
        compiler_params=pltpu.CompilerParams(vmem_limit_bytes=58 * 2**20),
        name="attend",
    )(lengths, page_table, selected.T, queries.reshape(rows, channels), pool)


def merge(mine, theirs, latent):
    top_lane = lax.broadcasted_iota(jnp.int32, mine.shape, 2) == latent
    mine_top, their_top = mine[:, :, latent : latent + 1], theirs[:, :, latent : latent + 1]
    top = jnp.maximum(mine_top, their_top)
    both = mine * jnp.exp(mine_top - top) + theirs * jnp.exp(their_top - top)
    return jnp.where(top_lane, top, both)


def local(queries, kv_pages, page_table, lengths, selected):
    latent = queries.shape[2] - ROPE
    devices = lax.axis_size("head")
    strides = [1 << b for b in reversed(range(devices.bit_length() - 1))]

    def swap(x, stride):
        return lax.ppermute(x, "head", [(i, i ^ stride) for i in range(devices)])

    gathered = queries.transpose(1, 0, 2)
    for stride in strides:
        gathered = jnp.concatenate([gathered, swap(gathered, stride)], axis=0)
    part = attend(
        gathered.transpose(1, 0, 2), kv_pages.transpose(1, 2, 0), page_table, lengths, selected
    ).transpose(1, 0, 2)
    for stride in reversed(strides):
        half = part.shape[0] // 2
        part = merge(part[:half], swap(part[half:], stride), latent)
    out = part[0, :, :latent] / part[0, :, latent + 1 : latent + 2]
    return out.astype(jnp.bfloat16)[:, None, :]


def solution(mesh):
    return jax.shard_map(
        local,
        mesh=mesh,
        in_specs=(
            P("grp", "head", None),
            P(("grp", "head"), None, None),
            P("grp", None),
            P("grp"),
            P("grp", None),
        ),
        out_specs=P("grp", "head", None),
        check_vma=False,
    )
```

```python
import functools
import math

import jax
import jax.numpy as jnp
from jax import lax
from jax.experimental import pallas as pl
from jax.experimental.pallas import tpu as pltpu
from jax.sharding import PartitionSpec as P

ROPE = 64
LANES = 128
NEG = -1e30
NARROW = 1
CHUNK = 32

SOFTMAX_SCALE = (0.1 * math.log(40.0) + 1.0) ** 2 / math.sqrt(192.0)

VMEM = pl.BlockSpec(memory_space=pltpu.VMEM)
SMEM = pl.BlockSpec(memory_space=pltpu.SMEM)
HBM = pl.BlockSpec(memory_space=pltpu.HBM)


def in_hbm(x):
    return pltpu.with_memory_space_constraint(x, pltpu.HBM)


def plan_kernel(
    tokens, lengths_hbm, table_hbm, picks_hbm, own_hbm, owner_ref, count_ref, tiles_ref, own_ref,
    lengths_ref, table_ref, picks_ref, sems,
):
    copies = [
        pltpu.make_async_copy(src, dst, sems.at[i])
        for i, (src, dst) in enumerate(
            [(picks_hbm, picks_ref), (table_hbm, table_ref), (lengths_hbm, lengths_ref), (own_hbm, own_ref)]
        )
    ]
    for copy in copies:
        copy.start()
    slots, _, width = owner_ref.shape
    reqs, blocks = table_ref.shape
    picks = picks_ref.shape[1]
    pool = slots * width
    first_page = lax.axis_index("head") * pool
    block_lane = lax.broadcasted_iota(jnp.int32, (picks, blocks), 1)
    pool_lane = lax.broadcasted_iota(jnp.int32, (picks, pool), 1)
    owner = jnp.zeros((picks, pool), jnp.float32)
    count = jnp.zeros((picks, pool), jnp.float32)
    for copy in copies[:3]:
        copy.wait()
    by_row = picks_ref[...].astype(jnp.float32).T.astype(jnp.int32)
    for r in range(reqs):
        pick = by_row[:, r : r + 1]
        row = table_ref[r : r + 1, :].astype(jnp.float32)
        page = jnp.sum(
            jnp.where(block_lane == pick, row, 0.0), axis=1, keepdims=True
        ).astype(jnp.int32)
        live = jnp.clip(lengths_ref[r] - pick * tokens, 0, tokens)
        hit = pool_lane == page - first_page
        owner = jnp.where(hit, float(r + 1), owner)
        count = jnp.where(hit, live.astype(jnp.float32), count)
    owner = jnp.sum(owner, axis=0, keepdims=True)
    count = jnp.sum(count, axis=0, keepdims=True).astype(jnp.int32)
    used = jnp.int32(0)
    for tile in range(slots):
        own = owner[:, tile * width : (tile + 1) * width]
        needed = jnp.max(own) > 0.5
        slot = used

        @pl.when(needed)
        def _(tile=tile, own=own, slot=slot):
            tiles_ref[1 + slot] = tile
            owner_ref[slot] = own.astype(jnp.int32) - 1
            count_ref[slot] = count[:, tile * width : (tile + 1) * width]

        used = used + needed.astype(jnp.int32)
    tiles_ref[0] = used
    copies[3].wait()


def plan(lengths, page_table, selected, queries, slots, width, tokens):
    return pl.pallas_call(
        functools.partial(plan_kernel, tokens),
        out_shape=(
            pltpu.VMEM((slots, 1, width), jnp.int32),
            pltpu.VMEM((slots, 1, width), jnp.int32),
            pltpu.SMEM((slots + 1,), jnp.int32),
            pltpu.VMEM(queries.shape, queries.dtype),
        ),
        in_specs=[HBM] * 4,
        out_specs=(VMEM, VMEM, SMEM, VMEM),
        scratch_shapes=[
            pltpu.SMEM(lengths.shape, jnp.int32),
            pltpu.VMEM(page_table.shape, jnp.int32),
            pltpu.VMEM(selected.shape, jnp.int32),
            pltpu.SemaphoreType.DMA((4,)),
        ],
        compiler_params=pltpu.CompilerParams(vmem_limit_bytes=2**21),
        name="plan",
    )(in_hbm(lengths), in_hbm(page_table), in_hbm(selected), in_hbm(queries))


def tile_copy(tiles_ref, pool_ref, pages_ref, sem, slot, first, tokens):
    width = pages_ref.shape[2]
    part = pool_ref.at[pl.ds(first, tokens)]
    if pool_ref.shape[2] > width:
        lane = pl.multiple_of(tiles_ref[1 + slot] * width, width)
        part = part.at[:, :, pl.ds(lane, width)]
    return pltpu.make_async_copy(part, pages_ref.at[pl.ds(first, tokens)], sem)


def fetch_kernel(first, tokens, tiles_ref, pool_ref, *refs):
    pages_ref, sem = refs[-2:]

    @pl.when(tiles_ref[0] > 0)
    def _():
        copy = tile_copy(tiles_ref, pool_ref, pages_ref, sem, 0, first, tokens)
        copy.start()
        copy.wait()


def fetch(tiles, pool, width, first, tokens, pages=None):
    more = [] if pages is None else [pages]
    return pl.pallas_call(
        functools.partial(fetch_kernel, first, tokens),
        out_shape=pltpu.VMEM((*pool.shape[:2], width), jnp.bfloat16),
        in_specs=[SMEM, HBM] + [VMEM] * len(more),
        out_specs=VMEM,
        scratch_shapes=[pltpu.SemaphoreType.DMA],
        input_output_aliases={2: 0} if more else {},
        compiler_params=pltpu.CompilerParams(vmem_limit_bytes=2**20),
        name=f"fetch{first}",
    )(tiles, pool, *more)


def by_request(owner_ref, values_ref, used, reqs, join, empty):
    def step(slot, joined):
        own, values = owner_ref[slot], values_ref[slot]
        return tuple(join(x, jnp.where(own == r, values, empty)) for r, x in enumerate(joined))

    start = jnp.full(values_ref.shape[1:], empty, jnp.float32)
    return lax.fori_loop(0, used, step, (start,) * reqs)


def attend_kernel(
    sizes, tiles_ref, owner_ref, count_ref, queries_ref, pool_ref, _, pages_ref, keep_ref, send_ref,
    scores, tops, sums, numer, sem,
):
    reqs, heads, latent, chunk = sizes
    tokens, channels, width = pages_ref.shape
    group = 2 if width == LANES else 1
    used = tiles_ref[0]

    def reload(slot):
        copy = tile_copy(tiles_ref, pool_ref, pages_ref, sem, slot, 0, tokens)
        copy.start()
        copy.wait()

    @pl.loop(0, used)
    def _(slot):
        @pl.when(slot > 0)
        def _():
            reload(slot)

        own, live = owner_ref[slot], count_ref[slot]
        own_wide = jnp.concatenate([own] * group, axis=1)
        tops[slot] = jnp.full((heads, width), NEG, jnp.float32)

        @pl.loop(0, tokens // chunk)
        def _(part):
            top = tops[slot]
            for t in range(0, chunk, group):
                token = part * chunk + t
                both = jnp.dot(
                    queries_ref[...],
                    jnp.concatenate([pages_ref[token + g] for g in range(group)], axis=1),
                    preferred_element_type=jnp.float32,
                )
                mine = both[:heads]
                for r in range(1, reqs):
                    mine = jnp.where(own_wide == r, both[r * heads : (r + 1) * heads], mine)
                for g in range(group):
                    score = mine[:, g * width : (g + 1) * width] * SOFTMAX_SCALE
                    score = jnp.where(live > token + g, score, NEG)
                    scores[slot, token + g] = score
                    top = jnp.maximum(top, score)
            tops[slot] = top

    row_top = [jnp.max(x, axis=1, keepdims=True) for x in by_request(owner_ref, tops, used, reqs, jnp.maximum, NEG)]
    numer[...] = jnp.zeros(numer.shape, jnp.float32)

    @pl.loop(0, used)
    def _(step):
        slot = used - 1 - step

        @pl.when(step > 0)
        def _():
            reload(slot)

        own, live = owner_ref[slot], count_ref[slot]
        shift = jnp.zeros((heads, width), jnp.float32)
        for r in range(reqs):
            shift = jnp.where(own == r, row_top[r], shift)
        sums[slot] = jnp.zeros((heads, width), jnp.float32)

        @pl.loop(0, tokens // chunk)
        def _(part):
            acc = sums[slot]
            weights, values = [], []
            for t in range(chunk):
                token = part * chunk + t
                weight = jnp.where(live > token, jnp.exp(scores[slot, token] - shift), 0.0)
                acc = acc + weight
                spread = [jnp.where(own == r, weight, 0.0).astype(jnp.bfloat16) for r in range(reqs)]
                weights.append(jnp.concatenate(spread, axis=0))
                values.append(pages_ref[token, :latent])
            sums[slot] = acc
            numer[...] += lax.dot_general(
                jnp.concatenate(weights, axis=1),
                jnp.concatenate(values, axis=1),
                (((1,), (1,)), ((), ())),
                preferred_element_type=jnp.float32,
            )

    cut = heads // 2
    totals = by_request(owner_ref, sums, used, reqs, jnp.add, 0.0)
    for r in range(reqs):
        total = jnp.sum(totals[r], axis=1, keepdims=True)
        last = tail_of(row_top[r], total, jnp.float32)
        for ref, first in ((keep_ref, 0), (send_ref, cut)):
            rows = pl.ds(r, cut, stride=reqs)
            mine = numer[r * heads + first : r * heads + first + cut]
            for i in range(latent // LANES):
                ref.at[i][rows, :] = mine[:, i * LANES : (i + 1) * LANES]
            ref.at[latent // LANES][rows, :] = last[first : first + cut]


def attend(queries, pages, pool, owner, count, tiles):
    reqs, heads, channels = queries.shape
    slots = owner.shape[0]
    tokens, _, width = pages.shape
    latent = channels - ROPE
    chunk = math.gcd(CHUNK, tokens)
    rows = reqs * heads
    half = pltpu.VMEM((latent // LANES + 1, rows // 2, LANES), jnp.float32)
    _, keep, send = pl.pallas_call(
        functools.partial(attend_kernel, (reqs, heads, latent, chunk)),
        out_shape=(pltpu.VMEM(pages.shape, pages.dtype), half, half),
        in_specs=[SMEM] + [VMEM] * 3 + [HBM, VMEM],
        out_specs=(VMEM,) * 3,
        scratch_shapes=[
            pltpu.VMEM((slots, tokens, heads, width), jnp.float32),
            pltpu.VMEM((slots, heads, width), jnp.float32),
            pltpu.VMEM((slots, heads, width), jnp.float32),
            pltpu.VMEM((rows, latent), jnp.float32),
            pltpu.SemaphoreType.DMA,
        ],
        input_output_aliases={5: 0},
        compiler_params=pltpu.CompilerParams(vmem_limit_bytes=(24 if heads > 16 else 12) * 2**20),
        name="attend",
    )(tiles, owner, count, queries.reshape(rows, channels), pool, pages)
    return keep, send


def tail_of(top, total, dtype):
    lane = lax.broadcasted_iota(jnp.int32, (*top.shape[:-1], LANES), top.ndim - 1)
    tail = jnp.zeros(lane.shape, jnp.float32)
    terms = []
    for value in (top, total):
        for _ in range(1 if dtype == jnp.float32 else 3):
            term = value.astype(dtype).astype(jnp.float32)
            terms.append(term)
            value = value - term
    for i, term in enumerate(terms):
        tail = jnp.where(lane == i, term, tail)
    return tail.astype(dtype)


def split_tail(tail):
    wide = tail.astype(jnp.float32)
    count = 1 if tail.dtype == jnp.float32 else 3
    parts = [wide[..., i : i + 1] for i in range(2 * count)]
    return sum(parts[1:count], parts[0]), sum(parts[count + 1 :], parts[count])


def combine(mine_ref, theirs_ref, rows):
    mine_top, mine_total = split_tail(mine_ref[mine_ref.shape[0] - 1, rows])
    their_top, their_total = split_tail(theirs_ref[theirs_ref.shape[0] - 1, rows])
    top = jnp.maximum(mine_top, their_top)
    mine_scale, their_scale = jnp.exp(mine_top - top), jnp.exp(their_top - top)
    numer = [
        mine_ref[i, rows] * mine_scale + theirs_ref[i, rows].astype(jnp.float32) * their_scale
        for i in range(mine_ref.shape[0] - 1)
    ]
    return numer, top, mine_total * mine_scale + their_total * their_scale


def merge_kernel(mine_ref, theirs_ref, keep_ref, send_ref):
    cut = keep_ref.shape[1]
    for rows, ref in ((pl.ds(cut, cut), send_ref), (pl.ds(0, cut), keep_ref)):
        numer, top, total = combine(mine_ref, theirs_ref, rows)
        for i, value in enumerate(numer):
            ref[i] = value.astype(ref.dtype)
        ref[len(numer)] = tail_of(top, total, ref.dtype)


def finish_kernel(mine_ref, theirs_ref, out_ref):
    numer, _, total = combine(mine_ref, theirs_ref, slice(None))
    for i, value in enumerate(numer):
        out_ref[:, i * LANES : (i + 1) * LANES] = (value / total).astype(out_ref.dtype)


def merge(mine, theirs, wire):
    tiles, rows, _ = mine.shape
    half = (tiles, rows // 2, LANES)
    return pl.pallas_call(
        merge_kernel,
        out_shape=(pltpu.VMEM(half, jnp.float32), pltpu.VMEM(half, wire)),
        in_specs=[VMEM, VMEM],
        out_specs=(VMEM, VMEM),
        compiler_params=pltpu.CompilerParams(vmem_limit_bytes=2**21),
        name=f"merge{rows}",
    )(mine, theirs)


def finish(mine, theirs):
    tiles, rows, _ = mine.shape
    return pl.pallas_call(
        finish_kernel,
        out_shape=jax.ShapeDtypeStruct((rows, (tiles - 1) * LANES), jnp.bfloat16),
        in_specs=[VMEM, VMEM],
        out_specs=VMEM,
        compiler_params=pltpu.CompilerParams(vmem_limit_bytes=2**20),
        name="finish",
    )(mine, theirs)


def local(queries, kv_pages, page_table, lengths, selected):
    pages_dev, tokens = kv_pages.shape[:2]
    devices = lax.axis_size("head")
    strides = [1 << b for b in reversed(range(devices.bit_length() - 1))]
    width = LANES if pages_dev % LANES == 0 else pages_dev
    slots = pages_dev // width

    def swap(x, stride):
        return lax.ppermute(x, "head", [(i, i ^ stride) for i in range(devices)])

    pool = in_hbm(kv_pages.transpose(1, 2, 0))
    asked = queries.transpose(1, 0, 2)
    owner, count, tiles, own = plan(lengths, page_table, selected, asked, slots, width, tokens)
    gathered = jnp.concatenate([own, swap(asked, strides[0])], axis=0)
    pages, first = None, 0
    for stride in strides[1:]:
        gathered = lax.optimization_barrier(gathered)
        arriving = swap(gathered, stride)
        if first < tokens:
            pages = fetch(tiles, pool, width, first, tokens // 2, pages)
            first += tokens // 2
            gathered, pages = lax.optimization_barrier((gathered, pages))
        gathered = jnp.concatenate([gathered, arriving], axis=0)
    keep, send = attend(gathered.transpose(1, 0, 2), pages, pool, owner, count, tiles)
    for i, stride in enumerate(reversed(strides[1:])):
        keep, send = merge(keep, swap(send, stride), jnp.bfloat16 if i < NARROW else jnp.float32)
    return finish(keep, swap(send, strides[0]))[:, None, :]


def solution(mesh):
    return jax.shard_map(
        local,
        mesh=mesh,
        in_specs=(
            P("grp", "head", None),
            P(("grp", "head"), None, None),
            P("grp", None),
            P("grp"),
            P("grp", None),
        ),
        out_specs=P("grp", "head", None),
        check_vma=False,
    )
```

```python
import functools
import math

import jax
import jax.numpy as jnp
from jax import lax
from jax.experimental import pallas as pl
from jax.experimental.pallas import tpu as pltpu
from jax.sharding import PartitionSpec as P

ROPE = 64
LANES = 128
NEG = -1e30
WIRES = (jnp.bfloat16, jnp.bfloat16, jnp.bfloat16)
CHUNK = 32

SOFTMAX_SCALE = (0.1 * math.log(40.0) + 1.0) ** 2 / math.sqrt(192.0)

VMEM = pl.BlockSpec(memory_space=pltpu.VMEM)
SMEM = pl.BlockSpec(memory_space=pltpu.SMEM)
HBM = pl.BlockSpec(memory_space=pltpu.HBM)


def in_hbm(x):
    return pltpu.with_memory_space_constraint(x, pltpu.HBM)


def plan_kernel(
    tokens, lengths_hbm, table_hbm, picks_hbm, own_hbm, owner_ref, count_ref, tiles_ref, own_ref,
    lengths_ref, table_ref, picks_ref, sems,
):
    copies = [
        pltpu.make_async_copy(src, dst, sems.at[i])
        for i, (src, dst) in enumerate(
            [(picks_hbm, picks_ref), (table_hbm, table_ref), (lengths_hbm, lengths_ref), (own_hbm, own_ref)]
        )
    ]
    for copy in copies:
        copy.start()
    slots, _, width = owner_ref.shape
    reqs, blocks = table_ref.shape
    picks = picks_ref.shape[1]
    pool = slots * width
    first_page = lax.axis_index("head") * pool
    block_lane = lax.broadcasted_iota(jnp.int32, (picks, blocks), 1)
    page_lane = first_page + lax.broadcasted_iota(jnp.int32, (picks, pool), 1)
    bits = tokens.bit_length()
    for copy in copies[:3]:
        copy.wait()
    by_row = picks_ref[...].astype(jnp.float32).T.astype(jnp.int32)
    code = jnp.zeros((picks, pool), jnp.int32)
    for r in range(reqs):
        pick = by_row[:, r : r + 1]
        row = table_ref[r : r + 1, :].astype(jnp.float32)
        page = jnp.sum(
            jnp.where(block_lane == pick, row, 0.0), axis=1, keepdims=True
        ).astype(jnp.int32)
        live = jnp.clip(lengths_ref[r] - pick * tokens, 0, tokens)
        code = jnp.where(page_lane == page, live + ((r + 1) << bits), code)
    code = jnp.sum(code, axis=0, keepdims=True)
    owner, count = (code >> bits).astype(jnp.float32), code & ((1 << bits) - 1)
    used = jnp.int32(0)
    for tile in range(slots):
        own = owner[:, tile * width : (tile + 1) * width]
        needed = jnp.max(own) > 0.5
        slot = used

        @pl.when(needed)
        def _(tile=tile, own=own, slot=slot):
            tiles_ref[1 + slot] = tile
            owner_ref[slot] = own.astype(jnp.int32) - 1
            count_ref[slot] = count[:, tile * width : (tile + 1) * width]

        used = used + needed.astype(jnp.int32)
    tiles_ref[0] = used
    copies[3].wait()


def plan(lengths, page_table, selected, queries, slots, width, tokens):
    return pl.pallas_call(
        functools.partial(plan_kernel, tokens),
        out_shape=(
            pltpu.VMEM((slots, 1, width), jnp.int32),
            pltpu.VMEM((slots, 1, width), jnp.int32),
            pltpu.SMEM((slots + 1,), jnp.int32),
            pltpu.VMEM(queries.shape, queries.dtype),
        ),
        in_specs=[HBM] * 4,
        out_specs=(VMEM, VMEM, SMEM, VMEM),
        scratch_shapes=[
            pltpu.SMEM(lengths.shape, jnp.int32),
            pltpu.VMEM(page_table.shape, jnp.int32),
            pltpu.VMEM(selected.shape, jnp.int32),
            pltpu.SemaphoreType.DMA((4,)),
        ],
        compiler_params=pltpu.CompilerParams(vmem_limit_bytes=2**21),
        name="plan",
    )(in_hbm(lengths), in_hbm(page_table), in_hbm(selected), in_hbm(queries))


def head_start(tokens):
    chunk = math.gcd(CHUNK, tokens)
    return chunk + (tokens - chunk) // 4


def tile_copy(tiles_ref, pool_ref, pages_ref, sem, slot, first, tokens):
    width = pages_ref.shape[2]
    part = pool_ref.at[pl.ds(first, tokens)]
    if pool_ref.shape[2] > width:
        lane = pl.multiple_of(tiles_ref[1 + slot] * width, width)
        part = part.at[:, :, pl.ds(lane, width)]
    return pltpu.make_async_copy(part, pages_ref.at[pl.ds(first, tokens)], sem)


def fetch_kernel(first, tokens, tiles_ref, pool_ref, *refs):
    pages_ref, sem = refs[-2:]

    @pl.when(tiles_ref[0] > 0)
    def _():
        copy = tile_copy(tiles_ref, pool_ref, pages_ref, sem, 0, first, tokens)
        copy.start()
        copy.wait()


def fetch(tiles, pool, width, first, tokens, pages=None):
    more = [] if pages is None else [pages]
    return pl.pallas_call(
        functools.partial(fetch_kernel, first, tokens),
        out_shape=pltpu.VMEM((*pool.shape[:2], width), jnp.bfloat16),
        in_specs=[SMEM, HBM] + [VMEM] * len(more),
        out_specs=VMEM,
        scratch_shapes=[pltpu.SemaphoreType.DMA],
        input_output_aliases={2: 0} if more else {},
        compiler_params=pltpu.CompilerParams(vmem_limit_bytes=2**20),
        name=f"fetch{first}",
    )(tiles, pool, *more)


def by_request(owner_ref, values_ref, used, reqs, join, empty):
    def step(slot, joined):
        own, values = owner_ref[slot], values_ref[slot]
        return tuple(join(x, jnp.where(own == r, values, empty)) for r, x in enumerate(joined))

    start = jnp.full(values_ref.shape[1:], empty, jnp.float32)
    return lax.fori_loop(0, used, step, (start,) * reqs)


def attend_kernel(
    sizes, tiles_ref, owner_ref, count_ref, queries_ref, pool_ref, _, pages_ref, keep_ref, send_ref,
    scores, tops, sums, numer, sem,
):
    reqs, heads, latent, chunk = sizes
    tokens, channels, width = pages_ref.shape
    group = 2 if width == LANES else 1
    used = tiles_ref[0]

    def reload(slot):
        copy = tile_copy(tiles_ref, pool_ref, pages_ref, sem, slot, 0, tokens)
        copy.start()
        copy.wait()

    ahead = head_start(tokens)
    rest = tile_copy(tiles_ref, pool_ref, pages_ref, sem, 0, ahead, tokens - ahead)

    @pl.when(used > 0)
    def _():
        rest.start()

    @pl.loop(0, used)
    def _(slot):
        @pl.when(slot > 0)
        def _():
            reload(slot)

        own, live = owner_ref[slot], count_ref[slot]
        own_wide = jnp.concatenate([own] * group, axis=1)
        tops[slot] = jnp.full((heads, width), NEG, jnp.float32)

        @pl.loop(0, tokens // chunk)
        def _(part):
            @pl.when((slot == 0) & (part == 1))
            def _():
                rest.wait()

            top = tops[slot]
            for t in range(0, chunk, group):
                token = part * chunk + t
                both = jnp.dot(
                    queries_ref[...],
                    jnp.concatenate([pages_ref[token + g] for g in range(group)], axis=1),
                    preferred_element_type=jnp.float32,
                )
                mine = both[:heads]
                for r in range(1, reqs):
                    mine = jnp.where(own_wide == r, both[r * heads : (r + 1) * heads], mine)
                for g in range(group):
                    score = mine[:, g * width : (g + 1) * width] * SOFTMAX_SCALE
                    score = jnp.where(live > token + g, score, NEG)
                    scores[slot, token + g] = score
                    top = jnp.maximum(top, score)
            tops[slot] = top

    row_top = [jnp.max(x, axis=1, keepdims=True) for x in by_request(owner_ref, tops, used, reqs, jnp.maximum, NEG)]
    numer[...] = jnp.zeros(numer.shape, jnp.float32)

    @pl.loop(0, used)
    def _(step):
        slot = used - 1 - step

        @pl.when(step > 0)
        def _():
            reload(slot)

        own, live = owner_ref[slot], count_ref[slot]
        shift = jnp.zeros((heads, width), jnp.float32)
        for r in range(reqs):
            shift = jnp.where(own == r, row_top[r], shift)
        sums[slot] = jnp.zeros((heads, width), jnp.float32)

        @pl.loop(0, tokens // chunk)
        def _(part):
            acc = sums[slot]
            weights, values = [], []
            for t in range(chunk):
                token = part * chunk + t
                weight = jnp.where(live > token, jnp.exp(scores[slot, token] - shift), 0.0)
                acc = acc + weight
                spread = [jnp.where(own == r, weight, 0.0).astype(jnp.bfloat16) for r in range(reqs)]
                weights.append(jnp.concatenate(spread, axis=0))
                values.append(pages_ref[token, :latent])
            sums[slot] = acc
            numer[...] += lax.dot_general(
                jnp.concatenate(weights, axis=1),
                jnp.concatenate(values, axis=1),
                (((1,), (1,)), ((), ())),
                preferred_element_type=jnp.float32,
            )

    cut = heads // 2
    totals = by_request(owner_ref, sums, used, reqs, jnp.add, 0.0)
    for r in range(reqs):
        total = jnp.sum(totals[r], axis=1, keepdims=True)
        last = tail_of(row_top[r], total, jnp.float32)
        for ref, first in ((keep_ref, 0), (send_ref, cut)):
            rows = pl.ds(r, cut, stride=reqs)
            mine = numer[r * heads + first : r * heads + first + cut]
            for i in range(latent // LANES):
                ref.at[i][rows, :] = mine[:, i * LANES : (i + 1) * LANES]
            ref.at[latent // LANES][rows, :] = last[first : first + cut]


def attend(queries, pages, pool, owner, count, tiles):
    reqs, heads, channels = queries.shape
    slots = owner.shape[0]
    tokens, _, width = pages.shape
    latent = channels - ROPE
    chunk = math.gcd(CHUNK, tokens)
    assert chunk < tokens
    rows = reqs * heads
    half = pltpu.VMEM((latent // LANES + 1, rows // 2, LANES), jnp.float32)
    _, keep, send = pl.pallas_call(
        functools.partial(attend_kernel, (reqs, heads, latent, chunk)),
        out_shape=(pltpu.VMEM(pages.shape, pages.dtype), half, half),
        in_specs=[SMEM] + [VMEM] * 3 + [HBM, VMEM],
        out_specs=(VMEM,) * 3,
        scratch_shapes=[
            pltpu.VMEM((slots, tokens, heads, width), jnp.float32),
            pltpu.VMEM((slots, heads, width), jnp.float32),
            pltpu.VMEM((slots, heads, width), jnp.float32),
            pltpu.VMEM((rows, latent), jnp.float32),
            pltpu.SemaphoreType.DMA,
        ],
        input_output_aliases={5: 0},
        compiler_params=pltpu.CompilerParams(vmem_limit_bytes=(24 if heads > 16 else 12) * 2**20),
        name="attend",
    )(tiles, owner, count, queries.reshape(rows, channels), pool, pages)
    return keep, send


def tail_of(top, total, dtype):
    lane = lax.broadcasted_iota(jnp.int32, (*top.shape[:-1], LANES), top.ndim - 1)
    tail = jnp.zeros(lane.shape, jnp.float32)
    terms = []
    for value in (top, total):
        for _ in range(1 if dtype == jnp.float32 else 3):
            term = value.astype(dtype).astype(jnp.float32)
            terms.append(term)
            value = value - term
    for i, term in enumerate(terms):
        tail = jnp.where(lane == i, term, tail)
    return tail.astype(dtype)


def split_tail(tail):
    wide = tail.astype(jnp.float32)
    count = 1 if tail.dtype == jnp.float32 else 3
    parts = [wide[..., i : i + 1] for i in range(2 * count)]
    return sum(parts[1:count], parts[0]), sum(parts[count + 1 :], parts[count])


def combine(refs, rows):
    last = refs[0].shape[0] - 1
    tops, totals = zip(*[split_tail(ref[last, rows]) for ref in refs])
    top = functools.reduce(jnp.maximum, tops)
    scales = [jnp.exp(x - top) for x in tops]
    numer = [
        sum(ref[i, rows].astype(jnp.float32) * scale for ref, scale in zip(refs, scales))
        for i in range(last)
    ]
    return numer, top, sum(total * scale for total, scale in zip(totals, scales))


def merge_kernel(mine_ref, theirs_ref, *out_refs):
    cut = out_refs[0].shape[1]
    for part, ref in reversed(list(enumerate(out_refs))):
        numer, top, total = combine((mine_ref, theirs_ref), pl.ds(part * cut, cut))
        for i, value in enumerate(numer):
            ref[i] = value.astype(ref.dtype)
        ref[len(numer)] = tail_of(top, total, ref.dtype)


def finish_kernel(*refs):
    *refs, out_ref = refs
    numer, _, total = combine(refs, slice(None))
    for i, value in enumerate(numer):
        out_ref[:, i * LANES : (i + 1) * LANES] = (value / total).astype(out_ref.dtype)


def merge(mine, theirs, wires):
    tiles, rows, _ = mine.shape
    part = (tiles, rows // (1 + len(wires)), LANES)
    return pl.pallas_call(
        merge_kernel,
        out_shape=tuple(pltpu.VMEM(part, dtype) for dtype in (jnp.float32, *wires)),
        in_specs=[VMEM, VMEM],
        out_specs=(VMEM,) * (1 + len(wires)),
        compiler_params=pltpu.CompilerParams(vmem_limit_bytes=2**21),
        name=f"merge{rows}",
    )(mine, theirs)


def finish(*parts):
    tiles, rows, _ = parts[0].shape
    return pl.pallas_call(
        finish_kernel,
        out_shape=jax.ShapeDtypeStruct((rows, (tiles - 1) * LANES), jnp.bfloat16),
        in_specs=[VMEM] * len(parts),
        out_specs=VMEM,
        compiler_params=pltpu.CompilerParams(vmem_limit_bytes=2**20),
        name="finish",
    )(*parts)


def local(queries, kv_pages, page_table, lengths, selected):
    pages_dev, tokens = kv_pages.shape[:2]
    devices = lax.axis_size("head")
    strides = [1 << b for b in reversed(range(devices.bit_length() - 1))]
    width = LANES if pages_dev % LANES == 0 else pages_dev
    slots = pages_dev // width

    def swap(x, offset):
        return lax.ppermute(x, "head", [(i, i ^ offset) for i in range(devices)])

    pool = in_hbm(kv_pages.transpose(1, 2, 0))
    asked = queries.transpose(1, 0, 2)
    far = [strides[0], strides[1], strides[0] ^ strides[1]]
    arriving = [swap(asked, offset) for offset in far]
    owner, count, tiles, own = plan(lengths, page_table, selected, asked, slots, width, tokens)
    gathered = jnp.concatenate([own, *arriving], axis=0)
    for i, stride in enumerate(strides[2:]):
        gathered = lax.optimization_barrier(gathered)
        arriving = swap(gathered, stride)
        if i == 0:
            pages = fetch(tiles, pool, width, 0, head_start(tokens))
            gathered, pages = lax.optimization_barrier((gathered, pages))
        gathered = jnp.concatenate([gathered, arriving], axis=0)
    keep, send = attend(gathered.transpose(1, 0, 2), pages, pool, owner, count, tiles)
    near = list(reversed(strides[2:]))
    for stride in near[:-1]:
        keep, send = merge(keep, swap(send, stride), [jnp.bfloat16])
    keep, *sends = merge(keep, swap(send, near[-1]), WIRES)
    got = [swap(x, offset) for x, offset in reversed(list(zip(sends, far)))]
    return finish(keep, *got)[:, None, :]


def solution(mesh):
    return jax.shard_map(
        local,
        mesh=mesh,
        in_specs=(
            P("grp", "head", None),
            P(("grp", "head"), None, None),
            P("grp", None),
            P("grp"),
            P("grp", None),
        ),
        out_specs=P("grp", "head", None),
        check_vma=False,
    )
```

```python
import functools
import math

import jax
import jax.numpy as jnp
from jax import lax
from jax.experimental import pallas as pl
from jax.experimental.pallas import tpu as pltpu
from jax.sharding import PartitionSpec as P

ROPE = 64
LANES = 128
NEG = -1e30
WIRES = (jnp.bfloat16, jnp.bfloat16, jnp.bfloat16)
CHUNK = 32

SOFTMAX_SCALE = (0.1 * math.log(40.0) + 1.0) ** 2 / math.sqrt(192.0)

VMEM = pl.BlockSpec(memory_space=pltpu.VMEM)
SMEM = pl.BlockSpec(memory_space=pltpu.SMEM)
HBM = pl.BlockSpec(memory_space=pltpu.HBM)


def in_hbm(x):
    return pltpu.with_memory_space_constraint(x, pltpu.HBM)


def plan_kernel(
    tokens, lengths_hbm, table_hbm, picks_hbm, own_hbm, owner_ref, count_ref, tiles_ref, own_ref,
    lengths_ref, table_ref, picks_ref, sems,
):
    copies = [
        pltpu.make_async_copy(src, dst, sems.at[i])
        for i, (src, dst) in enumerate(
            [(picks_hbm, picks_ref), (table_hbm, table_ref), (lengths_hbm, lengths_ref), (own_hbm, own_ref)]
        )
    ]
    for copy in copies:
        copy.start()
    slots, _, width = owner_ref.shape
    reqs, blocks = table_ref.shape
    picks = picks_ref.shape[1]
    pool = slots * width
    first_page = lax.axis_index("head") * pool
    block_lane = lax.broadcasted_iota(jnp.int32, (picks, blocks), 1).astype(jnp.float32)
    page_lane = (first_page + lax.broadcasted_iota(jnp.int32, (picks, pool), 1)).astype(jnp.float32)
    bits = tokens.bit_length()
    for copy in copies[:3]:
        copy.wait()
    pick_column = picks_ref[...].astype(jnp.float32).T
    live_column = jnp.clip(lengths_ref[...].astype(jnp.float32) - pick_column * tokens, 0.0, tokens)
    request = lax.broadcasted_iota(jnp.int32, (picks, reqs), 1)
    live_column = live_column + ((request + 1) << bits).astype(jnp.float32)
    table = table_ref[...].astype(jnp.float32)
    code = jnp.zeros((picks, pool), jnp.float32)
    for r in range(reqs):
        chosen = block_lane == pick_column[:, r : r + 1]
        page = jnp.sum(jnp.where(chosen, table[r : r + 1, :], 0.0), axis=1, keepdims=True)
        code = jnp.where(page_lane == page, live_column[:, r : r + 1], code)
    code = jnp.sum(code, axis=0, keepdims=True).astype(jnp.int32)
    owner, count = (code >> bits).astype(jnp.float32), code & ((1 << bits) - 1)
    held = [owner[:, tile * width : (tile + 1) * width] for tile in range(slots)]
    marks = [(jnp.max(own, axis=1, keepdims=True) > 0.5).astype(jnp.float32) * 2.0**i for i, own in enumerate(held)]
    marks = jnp.max(sum(marks)).astype(jnp.int32)
    used = jnp.int32(0)
    for tile, own in enumerate(held):
        needed = (marks >> tile) & 1
        slot = used

        @pl.when(needed == 1)
        def _(tile=tile, own=own, slot=slot):
            tiles_ref[1 + slot] = tile
            owner_ref[slot] = own.astype(jnp.int32) - 1
            count_ref[slot] = count[:, tile * width : (tile + 1) * width]

        used = used + needed
    tiles_ref[0] = used
    copies[3].wait()


def plan(lengths, page_table, selected, queries, slots, width, tokens):
    return pl.pallas_call(
        functools.partial(plan_kernel, tokens),
        out_shape=(
            pltpu.VMEM((slots, 1, width), jnp.int32),
            pltpu.VMEM((slots, 1, width), jnp.int32),
            pltpu.SMEM((slots + 1,), jnp.int32),
            pltpu.VMEM(queries.shape, queries.dtype),
        ),
        in_specs=[HBM] * 4,
        out_specs=(VMEM, VMEM, SMEM, VMEM),
        scratch_shapes=[
            pltpu.VMEM((1, *lengths.shape), jnp.int32),
            pltpu.VMEM(page_table.shape, jnp.int32),
            pltpu.VMEM(selected.shape, jnp.int32),
            pltpu.SemaphoreType.DMA((4,)),
        ],
        compiler_params=pltpu.CompilerParams(vmem_limit_bytes=2**21),
        name="plan",
    )(in_hbm(lengths[None, :]), in_hbm(page_table), in_hbm(selected), in_hbm(queries))


def tile_copy(tiles_ref, pool_ref, pages_ref, sem, slot, first, tokens):
    width = pages_ref.shape[2]
    part = pool_ref.at[pl.ds(first, tokens)]
    if pool_ref.shape[2] > width:
        lane = pl.multiple_of(tiles_ref[1 + slot] * width, width)
        part = part.at[:, :, pl.ds(lane, width)]
    return pltpu.make_async_copy(part, pages_ref.at[pl.ds(first, tokens)], sem)


def fetch_kernel(tokens, tiles_ref, pool_ref, pages_ref, sem):
    @pl.when(tiles_ref[0] > 0)
    def _():
        copy = tile_copy(tiles_ref, pool_ref, pages_ref, sem, 0, 0, tokens)
        copy.start()
        copy.wait()


def fetch(tiles, pool, width, tokens):
    return pl.pallas_call(
        functools.partial(fetch_kernel, tokens),
        out_shape=pltpu.VMEM((*pool.shape[:2], width), jnp.bfloat16),
        in_specs=[SMEM, HBM],
        out_specs=VMEM,
        scratch_shapes=[pltpu.SemaphoreType.DMA],
        compiler_params=pltpu.CompilerParams(vmem_limit_bytes=2**20),
        name="fetch",
    )(tiles, pool)


def by_request(owner_ref, values_ref, used, reqs, join, empty):
    def step(slot, joined):
        own, values = owner_ref[slot], values_ref[slot]
        return tuple(join(x, jnp.where(own == r, values, empty)) for r, x in enumerate(joined))

    start = jnp.full(values_ref.shape[1:], empty, jnp.float32)
    return lax.fori_loop(0, used, step, (start,) * reqs)


def stack_rope(reqs, queries_ref, stacked):
    rows, channels = queries_ref.shape
    heads, groups = rows // reqs, stacked.shape[1] // ROPE
    members = reqs // groups
    for r in range(reqs):
        group, member = r // members, r % members
        stacked[member * heads : (member + 1) * heads, group * ROPE : (group + 1) * ROPE] = queries_ref[
            r * heads : (r + 1) * heads, channels - ROPE :
        ].astype(jnp.float32)
    return stacked[...].astype(jnp.bfloat16)


def pick_rows(choice, values, heads, count):
    mine = values[:heads]
    for i in range(1, count):
        mine = jnp.where(choice == i, values[i * heads : (i + 1) * heads], mine)
    return mine


def score_tiles(reqs, refs, prepare):
    tiles_ref, owner_ref, count_ref, queries_ref, pages_ref, scores, tops, stacked = refs
    tokens, channels, width = pages_ref.shape
    latent = channels - ROPE
    heads = queries_ref.shape[0] // reqs
    groups = stacked.shape[1] // ROPE
    members = reqs // groups
    chunk = math.gcd(CHUNK, tokens)
    pair = 2 if width == LANES else 1
    turned = stack_rope(reqs, queries_ref, stacked)

    @pl.loop(0, tiles_ref[0])
    def _(slot):
        own, live = owner_ref[slot], count_ref[slot]
        own_wide = jnp.concatenate([own] * pair, axis=1)
        member, group = own_wide & (members - 1), own_wide >> (members.bit_length() - 1)
        in_group = [(group == g).astype(jnp.float32).astype(jnp.bfloat16) for g in range(groups)]
        tops[slot] = jnp.full((heads, width), NEG, jnp.float32)

        @pl.loop(0, tokens // chunk)
        def _(part):
            prepare(slot, part)
            top = tops[slot]
            for t in range(0, chunk, pair):
                token = part * chunk + t
                keys = jnp.concatenate([pages_ref[token + g] for g in range(pair)], axis=1)
                by_latent = jnp.dot(
                    queries_ref[:, :latent], keys[:latent], preferred_element_type=jnp.float32
                )
                rope = keys[latent:]
                by_rope = jnp.dot(
                    turned,
                    jnp.concatenate([rope * inside for inside in in_group], axis=0),
                    preferred_element_type=jnp.float32,
                )
                mine = pick_rows(own_wide, by_latent, heads, reqs) + pick_rows(member, by_rope, heads, members)
                for g in range(pair):
                    score = mine[:, g * width : (g + 1) * width] * SOFTMAX_SCALE
                    score = jnp.where(live > token + g, score, NEG)
                    scores[slot, token + g] = score
                    top = jnp.maximum(top, score)
            tops[slot] = top


def weigh_tiles(reqs, refs, sets, prepare):
    tiles_ref, owner_ref, count_ref, pages_ref, numer = refs
    tokens, _, width = pages_ref.shape
    heads = sets[0][1].shape[1]
    chunk = tokens
    latent = numer.shape[1]
    used = tiles_ref[0]
    row_top = [
        [jnp.max(x, axis=1, keepdims=True) for x in by_request(owner_ref, tops, used, reqs, jnp.maximum, NEG)]
        for _, tops, _, _ in sets
    ]
    numer[...] = jnp.zeros(numer.shape, jnp.float32)

    @pl.loop(0, used)
    def _(slot):
        own, live = owner_ref[slot], count_ref[slot]
        shifts = []
        for row_tops, (_, _, sums, _) in zip(row_top, sets):
            shift = jnp.zeros((heads, width), jnp.float32)
            for r in range(reqs):
                shift = jnp.where(own == r, row_tops[r], shift)
            shifts.append(shift)
            sums[slot] = jnp.zeros((heads, width), jnp.float32)

        @pl.loop(0, tokens // chunk)
        def _(part):
            prepare(slot, part)
            acc = [sums[slot] for _, _, sums, _ in sets]
            weights, values = [], []
            for t in range(chunk):
                token = part * chunk + t
                spread = []
                for i, (scores, _, _, _) in enumerate(sets):
                    weight = jnp.where(live > token, jnp.exp(scores[slot, token] - shifts[i]), 0.0)
                    acc[i] = acc[i] + weight
                    spread += [jnp.where(own == r, weight, 0.0) for r in range(reqs)]
                weights.append(jnp.concatenate(spread, axis=0).astype(jnp.bfloat16))
                values.append(pages_ref[token, :latent])
            for x, (_, _, sums, _) in zip(acc, sets):
                sums[slot] = x
            numer[...] += lax.dot_general(
                jnp.concatenate(weights, axis=1),
                jnp.concatenate(values, axis=1),
                (((1,), (1,)), ((), ())),
                preferred_element_type=jnp.float32,
            )

    for n, (row_tops, (_, _, sums, out_refs)) in enumerate(zip(row_top, sets)):
        totals = by_request(owner_ref, sums, used, reqs, jnp.add, 0.0)
        cut = heads // len(out_refs)
        for r in range(reqs):
            last = tail_of(row_tops[r], jnp.sum(totals[r], axis=1, keepdims=True), jnp.float32)
            rows = pl.ds(r, cut, stride=reqs)
            for part, out_ref in enumerate(out_refs):
                first = (n * reqs + r) * heads + part * cut
                for i in range(latent // LANES):
                    out_ref.at[i][rows, :] = numer[first : first + cut, i * LANES : (i + 1) * LANES]
                out_ref.at[latent // LANES][rows, :] = last[part * cut : (part + 1) * cut]


def reload_tile(tiles_ref, pool_ref, pages_ref, sem):
    def prepare(slot, part):
        @pl.when((tiles_ref[0] > 1) & (part == 0))
        def _():
            copy = tile_copy(tiles_ref, pool_ref, pages_ref, sem, slot, 0, pages_ref.shape[0])
            copy.start()
            copy.wait()

    return prepare


def attend_kernel(
    reqs, ahead, tiles_ref, owner_ref, count_ref, queries_ref, pool_ref, _, pages_ref, keep_ref, send_ref,
    stacked, scores, tops, sums, numer, sem, rest_sem,
):
    tokens = pages_ref.shape[0]
    chunk = math.gcd(CHUNK, tokens)
    assert chunk < tokens and chunk <= ahead
    rest = tile_copy(tiles_ref, pool_ref, pages_ref, rest_sem, 0, ahead, tokens - ahead)
    reload = reload_tile(tiles_ref, pool_ref, pages_ref, sem)

    @pl.when(tiles_ref[0] > 0)
    def _():
        rest.start()

    def prepare(slot, part):
        @pl.when((slot == 0) & (part == jnp.where(tiles_ref[0] > 1, 0, 1)))
        def _():
            rest.wait()

        reload(slot, part)

    common = (tiles_ref, owner_ref, count_ref)
    score_tiles(reqs, (*common, queries_ref, pages_ref, scores, tops, stacked), prepare)
    sets = [(scores, tops, sums, (keep_ref, send_ref))]
    weigh_tiles(reqs, (*common, pages_ref, numer), sets, reload)


def attend(queries, pages, pool, plan, ahead):
    reqs, heads, channels = queries.shape
    owner, count, tiles = plan
    slots, _, width = owner.shape
    latent = channels - ROPE
    rows = reqs * heads
    out = pltpu.VMEM((latent // LANES + 1, rows // 2, LANES), jnp.float32)
    groups = max(g for g in (1, 2, 4) if reqs % g == 0)
    _, keep, send = pl.pallas_call(
        functools.partial(attend_kernel, reqs, ahead),
        out_shape=(pltpu.VMEM(pages.shape, pages.dtype), out, out),
        in_specs=[SMEM, VMEM, VMEM, VMEM, HBM, VMEM],
        out_specs=(VMEM,) * 3,
        scratch_shapes=[
            pltpu.VMEM((rows // groups, groups * ROPE), jnp.float32),
            pltpu.VMEM((slots, pages.shape[0], heads, width), jnp.float32),
            pltpu.VMEM((slots, heads, width), jnp.float32),
            pltpu.VMEM((slots, heads, width), jnp.float32),
            pltpu.VMEM((rows, latent), jnp.float32),
            pltpu.SemaphoreType.DMA,
            pltpu.SemaphoreType.DMA,
        ],
        input_output_aliases={5: 0},
        compiler_params=pltpu.CompilerParams(vmem_limit_bytes=40 * 2**20),
        name="attend",
    )(tiles, owner, count, queries.reshape(rows, channels), pool, pages)
    return keep, send


def tail_of(top, total, dtype):
    lane = lax.broadcasted_iota(jnp.int32, (*top.shape[:-1], LANES), top.ndim - 1)
    tail = jnp.zeros(lane.shape, jnp.float32)
    terms = []
    for value in (top, total):
        for _ in range(1 if dtype == jnp.float32 else 3):
            term = value.astype(dtype).astype(jnp.float32)
            terms.append(term)
            value = value - term
    for i, term in enumerate(terms):
        tail = jnp.where(lane == i, term, tail)
    return tail.astype(dtype)


def split_tail(tail):
    wide = tail.astype(jnp.float32)
    count = 1 if tail.dtype == jnp.float32 else 3
    parts = [wide[..., i : i + 1] for i in range(2 * count)]
    return sum(parts[1:count], parts[0]), sum(parts[count + 1 :], parts[count])


def combine(refs, rows):
    last = refs[0].shape[0] - 1
    tops, totals = zip(*[split_tail(ref[last, rows]) for ref in refs])
    top = functools.reduce(jnp.maximum, tops)
    scales = [jnp.exp(x - top) for x in tops]
    numer = [
        sum(ref[i, rows].astype(jnp.float32) * scale for ref, scale in zip(refs, scales))
        for i in range(last)
    ]
    return numer, top, sum(total * scale for total, scale in zip(totals, scales))


def merge_kernel(mine_ref, theirs_ref, *out_refs):
    cut = out_refs[0].shape[1]
    for part, ref in reversed(list(enumerate(out_refs))):
        numer, top, total = combine((mine_ref, theirs_ref), pl.ds(part * cut, cut))
        for i, value in enumerate(numer):
            ref[i] = value.astype(ref.dtype)
        ref[len(numer)] = tail_of(top, total, ref.dtype)


def finish_kernel(*refs):
    *refs, out_ref = refs
    numer, _, total = combine(refs, slice(None))
    for i, value in enumerate(numer):
        out_ref[:, i * LANES : (i + 1) * LANES] = (value / total).astype(out_ref.dtype)


def merge(mine, theirs, wires):
    tiles, rows, _ = mine.shape
    part = (tiles, rows // (1 + len(wires)), LANES)
    return pl.pallas_call(
        merge_kernel,
        out_shape=tuple(pltpu.VMEM(part, dtype) for dtype in (jnp.float32, *wires)),
        in_specs=[VMEM, VMEM],
        out_specs=(VMEM,) * (1 + len(wires)),
        compiler_params=pltpu.CompilerParams(vmem_limit_bytes=2**21),
        name=f"merge{rows}",
    )(mine, theirs)


def finish(*parts):
    tiles, rows, _ = parts[0].shape
    return pl.pallas_call(
        finish_kernel,
        out_shape=jax.ShapeDtypeStruct((rows, (tiles - 1) * LANES), jnp.bfloat16),
        in_specs=[VMEM] * len(parts),
        out_specs=VMEM,
        compiler_params=pltpu.CompilerParams(vmem_limit_bytes=2**20),
        name="finish",
    )(*parts)


def local(queries, kv_pages, page_table, lengths, selected):
    pages_dev, tokens = kv_pages.shape[:2]
    devices = lax.axis_size("head")
    strides = [1 << b for b in reversed(range(devices.bit_length() - 1))]
    width = LANES if pages_dev % LANES == 0 else pages_dev
    slots = pages_dev // width

    def swap(x, offset):
        return lax.ppermute(x, "head", [(i, i ^ offset) for i in range(devices)])

    pool = in_hbm(kv_pages.transpose(1, 2, 0))
    asked = queries.transpose(1, 0, 2)
    far = [strides[0], strides[1], strides[0] ^ strides[1]]
    arriving = [swap(asked, offset) for offset in far]
    owner, count, tiles, own = plan(lengths, page_table, selected, asked, slots, width, tokens)
    gathered = jnp.concatenate([own, *arriving], axis=0)
    ahead = tokens * 11 // 16
    for i, stride in enumerate(strides[2:]):
        gathered = lax.optimization_barrier(gathered)
        arriving = swap(gathered, stride)
        if i == 0:
            pages = fetch(tiles, pool, width, ahead)
            gathered, pages = lax.optimization_barrier((gathered, pages))
        gathered = jnp.concatenate([gathered, arriving], axis=0)
    keep, send = attend(gathered.transpose(1, 0, 2), pages, pool, (owner, count, tiles), ahead)
    theirs = swap(send, strides[-1])
    for stride in reversed(strides[3:-1]):
        keep, send = merge(keep, theirs, [jnp.bfloat16])
        theirs = swap(send, stride)
    keep, send = merge(keep, theirs, [jnp.bfloat16])
    keep, *sends = merge(keep, swap(send, strides[2]), WIRES)
    got = [swap(x, offset) for x, offset in reversed(list(zip(sends, far)))]
    return finish(keep, *got)[:, None, :]


def solution(mesh):
    return jax.shard_map(
        local,
        mesh=mesh,
        in_specs=(
            P("grp", "head", None),
            P(("grp", "head"), None, None),
            P("grp", None),
            P("grp"),
            P("grp", None),
        ),
        out_specs=P("grp", "head", None),
        check_vma=False,
    )
```

```python
import functools
import math

import jax
import jax.numpy as jnp
from jax import lax
from jax.experimental import pallas as pl
from jax.experimental.pallas import tpu as pltpu
from jax.sharding import PartitionSpec as P

ROPE = 64
LANES = 128
NEG = -1e30
WIRES = (jnp.bfloat16, jnp.bfloat16, jnp.bfloat16)
CHUNK = 32

SOFTMAX_SCALE = (0.1 * math.log(40.0) + 1.0) ** 2 / math.sqrt(192.0)

VMEM = pl.BlockSpec(memory_space=pltpu.VMEM)
SMEM = pl.BlockSpec(memory_space=pltpu.SMEM)
HBM = pl.BlockSpec(memory_space=pltpu.HBM)


def in_hbm(x):
    return pltpu.with_memory_space_constraint(x, pltpu.HBM)


def plan_kernel(
    tokens, lengths_hbm, table_hbm, picks_hbm, own_hbm, owner_ref, count_ref, tiles_ref, own_ref,
    lengths_ref, table_ref, picks_ref, sems,
):
    copies = [
        pltpu.make_async_copy(src, dst, sems.at[i])
        for i, (src, dst) in enumerate(
            [(picks_hbm, picks_ref), (table_hbm, table_ref), (lengths_hbm, lengths_ref), (own_hbm, own_ref)]
        )
    ]
    for copy in copies:
        copy.start()
    slots, _, width = owner_ref.shape
    reqs, blocks = table_ref.shape
    picks = picks_ref.shape[1]
    pool = slots * width
    first_page = lax.axis_index("head") * pool
    block_lane = lax.broadcasted_iota(jnp.int32, (picks, blocks), 1).astype(jnp.float32)
    page_lane = (first_page + lax.broadcasted_iota(jnp.int32, (picks, pool), 1)).astype(jnp.float32)
    bits = tokens.bit_length()
    for copy in copies[:3]:
        copy.wait()
    pick_column = picks_ref[...].astype(jnp.float32).T
    live_column = jnp.clip(lengths_ref[...].astype(jnp.float32) - pick_column * tokens, 0.0, tokens)
    request = lax.broadcasted_iota(jnp.int32, (picks, reqs), 1)
    live_column = live_column + ((request + 1) << bits).astype(jnp.float32)
    table = table_ref[...].astype(jnp.float32)
    code = jnp.zeros((picks, pool), jnp.float32)
    for r in range(reqs):
        chosen = block_lane == pick_column[:, r : r + 1]
        page = jnp.sum(jnp.where(chosen, table[r : r + 1, :], 0.0), axis=1, keepdims=True)
        code = jnp.where(page_lane == page, live_column[:, r : r + 1], code)
    code = jnp.sum(code, axis=0, keepdims=True).astype(jnp.int32)
    owner, count = (code >> bits).astype(jnp.float32), code & ((1 << bits) - 1)
    held = [owner[:, tile * width : (tile + 1) * width] for tile in range(slots)]
    marks = [(jnp.max(own, axis=1, keepdims=True) > 0.5).astype(jnp.float32) * 2.0**i for i, own in enumerate(held)]
    marks = jnp.max(sum(marks)).astype(jnp.int32)
    used = jnp.int32(0)
    for tile, own in enumerate(held):
        needed = (marks >> tile) & 1
        slot = used

        @pl.when(needed == 1)
        def _(tile=tile, own=own, slot=slot):
            tiles_ref[1 + slot] = tile
            owner_ref[slot] = own.astype(jnp.int32) - 1
            count_ref[slot] = count[:, tile * width : (tile + 1) * width]

        used = used + needed
    tiles_ref[0] = used
    copies[3].wait()


def plan(lengths, page_table, selected, queries, slots, width, tokens):
    return pl.pallas_call(
        functools.partial(plan_kernel, tokens),
        out_shape=(
            pltpu.VMEM((slots, 1, width), jnp.int32),
            pltpu.VMEM((slots, 1, width), jnp.int32),
            pltpu.SMEM((slots + 1,), jnp.int32),
            pltpu.VMEM(queries.shape, queries.dtype),
        ),
        in_specs=[HBM] * 4,
        out_specs=(VMEM, VMEM, SMEM, VMEM),
        scratch_shapes=[
            pltpu.VMEM((1, *lengths.shape), jnp.int32),
            pltpu.VMEM(page_table.shape, jnp.int32),
            pltpu.VMEM(selected.shape, jnp.int32),
            pltpu.SemaphoreType.DMA((4,)),
        ],
        compiler_params=pltpu.CompilerParams(vmem_limit_bytes=2**21),
        name="plan",
    )(in_hbm(lengths[None, :]), in_hbm(page_table), in_hbm(selected), in_hbm(queries))


def tile_copy(tiles_ref, pool_ref, pages_ref, sem, slot, first, tokens):
    width = pages_ref.shape[2]
    part = pool_ref.at[pl.ds(first, tokens)]
    if pool_ref.shape[2] > width:
        lane = pl.multiple_of(tiles_ref[1 + slot] * width, width)
        part = part.at[:, :, pl.ds(lane, width)]
    return pltpu.make_async_copy(part, pages_ref.at[pl.ds(first, tokens)], sem)


def fetch_kernel(tokens, tiles_ref, pool_ref, pages_ref, sem):
    @pl.when(tiles_ref[0] > 0)
    def _():
        copy = tile_copy(tiles_ref, pool_ref, pages_ref, sem, 0, 0, tokens)
        copy.start()
        copy.wait()


def fetch(tiles, pool, width, tokens):
    return pl.pallas_call(
        functools.partial(fetch_kernel, tokens),
        out_shape=pltpu.VMEM((*pool.shape[:2], width), jnp.bfloat16),
        in_specs=[SMEM, HBM],
        out_specs=VMEM,
        scratch_shapes=[pltpu.SemaphoreType.DMA],
        compiler_params=pltpu.CompilerParams(vmem_limit_bytes=2**20),
        name="fetch",
    )(tiles, pool)


def by_request(owner_ref, values_ref, used, reqs, join, empty):
    def step(slot, joined):
        own, values = owner_ref[slot], values_ref[slot]
        return tuple(join(x, jnp.where(own == r, values, empty)) for r, x in enumerate(joined))

    start = jnp.full(values_ref.shape[1:], empty, jnp.float32)
    return lax.fori_loop(0, used, step, (start,) * reqs)


def stack_rope(reqs, queries_ref, stacked):
    rows, channels = queries_ref.shape
    heads, groups = rows // reqs, stacked.shape[1] // ROPE
    members = reqs // groups
    for r in range(reqs):
        group, member = r // members, r % members
        stacked[member * heads : (member + 1) * heads, group * ROPE : (group + 1) * ROPE] = queries_ref[
            r * heads : (r + 1) * heads, channels - ROPE :
        ].astype(jnp.float32)
    return stacked[...].astype(jnp.bfloat16)


def pick_rows(choice, values, heads, count):
    mine = values[:heads]
    for i in range(1, count):
        mine = jnp.where(choice == i, values[i * heads : (i + 1) * heads], mine)
    return mine


def score_tiles(reqs, refs, prepare):
    tiles_ref, owner_ref, count_ref, queries_ref, pages_ref, scores, tops, stacked = refs
    tokens, channels, width = pages_ref.shape
    latent = channels - ROPE
    heads = queries_ref.shape[0] // reqs
    groups = stacked.shape[1] // ROPE
    members = reqs // groups
    chunk = math.gcd(CHUNK, tokens)
    pair = 2 if width == LANES else 1
    turned = stack_rope(reqs, queries_ref, stacked)

    @pl.loop(0, tiles_ref[0])
    def _(slot):
        own, live = owner_ref[slot], count_ref[slot]
        own_wide = jnp.concatenate([own] * pair, axis=1)
        member, group = own_wide & (members - 1), own_wide >> (members.bit_length() - 1)
        in_group = [(group == g).astype(jnp.float32).astype(jnp.bfloat16) for g in range(groups)]
        tops[slot] = jnp.full((heads, width), NEG, jnp.float32)

        @pl.loop(0, tokens // chunk)
        def _(part):
            prepare(slot, part)
            top = tops[slot]
            for t in range(0, chunk, pair):
                token = part * chunk + t
                keys = jnp.concatenate([pages_ref[token + g] for g in range(pair)], axis=1)
                by_latent = jnp.dot(
                    queries_ref[:, :latent], keys[:latent], preferred_element_type=jnp.float32
                )
                rope = keys[latent:]
                by_rope = jnp.dot(
                    turned,
                    jnp.concatenate([rope * inside for inside in in_group], axis=0),
                    preferred_element_type=jnp.float32,
                )
                mine = pick_rows(own_wide, by_latent, heads, reqs) + pick_rows(member, by_rope, heads, members)
                for g in range(pair):
                    score = mine[:, g * width : (g + 1) * width] * SOFTMAX_SCALE
                    score = jnp.where(live > token + g, score, NEG)
                    scores[slot, token + g] = score
                    top = jnp.maximum(top, score)
            tops[slot] = top


def weigh_tiles(reqs, refs, sets, prepare):
    tiles_ref, owner_ref, count_ref, pages_ref, numer = refs
    tokens, _, width = pages_ref.shape
    heads = sets[0][1].shape[1]
    chunk = tokens
    latent = numer.shape[1]
    used = tiles_ref[0]
    row_top = [
        [jnp.max(x, axis=1, keepdims=True) for x in by_request(owner_ref, tops, used, reqs, jnp.maximum, NEG)]
        for _, tops, _, _ in sets
    ]

    @pl.when(used == 0)
    def _():
        numer[...] = jnp.zeros(numer.shape, jnp.float32)

    @pl.loop(0, used)
    def _(slot):
        own, live = owner_ref[slot], count_ref[slot]
        shifts = []
        for row_tops, (_, _, sums, _) in zip(row_top, sets):
            shift = jnp.zeros((heads, width), jnp.float32)
            for r in range(reqs):
                shift = jnp.where(own == r, row_tops[r], shift)
            shifts.append(shift)
            sums[slot] = jnp.zeros((heads, width), jnp.float32)

        @pl.loop(0, tokens // chunk)
        def _(part):
            prepare(slot, part)
            acc = [sums[slot] for _, _, sums, _ in sets]
            weights, values = [], []
            for t in range(chunk):
                token = part * chunk + t
                spread = []
                for i, (scores, _, _, _) in enumerate(sets):
                    weight = jnp.where(live > token, jnp.exp(scores[slot, token] - shifts[i]), 0.0)
                    acc[i] = acc[i] + weight
                    spread += [jnp.where(own == r, weight, 0.0) for r in range(reqs)]
                weights.append(jnp.concatenate(spread, axis=0).astype(jnp.bfloat16))
                values.append(pages_ref[token, :latent])
            for x, (_, _, sums, _) in zip(acc, sets):
                sums[slot] = x
            numer[...] = jnp.where(slot == 0, 0.0, numer[...]) + lax.dot_general(
                jnp.concatenate(weights, axis=1),
                jnp.concatenate(values, axis=1),
                (((1,), (1,)), ((), ())),
                preferred_element_type=jnp.float32,
            )

    for n, (row_tops, (_, _, sums, out_refs)) in enumerate(zip(row_top, sets)):
        totals = by_request(owner_ref, sums, used, reqs, jnp.add, 0.0)
        cut = heads // len(out_refs)
        for r in range(reqs):
            last = tail_of(row_tops[r], jnp.sum(totals[r], axis=1, keepdims=True), jnp.float32)
            rows = pl.ds(r, cut, stride=reqs)
            for part, out_ref in enumerate(out_refs):
                first = (n * reqs + r) * heads + part * cut
                for i in range(latent // LANES):
                    out_ref.at[i][rows, :] = numer[first : first + cut, i * LANES : (i + 1) * LANES]
                out_ref.at[latent // LANES][rows, :] = last[part * cut : (part + 1) * cut]


def reload_tile(tiles_ref, pool_ref, pages_ref, sem):
    def prepare(slot, part):
        @pl.when((tiles_ref[0] > 1) & (part == 0))
        def _():
            copy = tile_copy(tiles_ref, pool_ref, pages_ref, sem, slot, 0, pages_ref.shape[0])
            copy.start()
            copy.wait()

    return prepare


def attend_kernel(
    reqs, ahead, tiles_ref, owner_ref, count_ref, queries_ref, pool_ref, _, pages_ref, keep_ref, send_ref,
    stacked, scores, tops, sums, numer, sem, rest_sem,
):
    tokens = pages_ref.shape[0]
    chunk = math.gcd(CHUNK, tokens)
    assert chunk < tokens and chunk <= ahead
    rest = tile_copy(tiles_ref, pool_ref, pages_ref, rest_sem, 0, ahead, tokens - ahead)
    reload = reload_tile(tiles_ref, pool_ref, pages_ref, sem)

    @pl.when(tiles_ref[0] > 0)
    def _():
        rest.start()

    def prepare(slot, part):
        @pl.when((slot == 0) & (part == jnp.where(tiles_ref[0] > 1, 0, 1)))
        def _():
            rest.wait()

        reload(slot, part)

    common = (tiles_ref, owner_ref, count_ref)
    score_tiles(reqs, (*common, queries_ref, pages_ref, scores, tops, stacked), prepare)
    sets = [(scores, tops, sums, (keep_ref, send_ref))]
    weigh_tiles(reqs, (*common, pages_ref, numer), sets, reload)


def attend(queries, pages, pool, plan, ahead):
    reqs, heads, channels = queries.shape
    owner, count, tiles = plan
    slots, _, width = owner.shape
    latent = channels - ROPE
    rows = reqs * heads
    out = pltpu.VMEM((latent // LANES + 1, rows // 2, LANES), jnp.float32)
    groups = max(g for g in (1, 2, 4) if reqs % g == 0)
    _, keep, send = pl.pallas_call(
        functools.partial(attend_kernel, reqs, ahead),
        out_shape=(pltpu.VMEM(pages.shape, pages.dtype), out, out),
        in_specs=[SMEM, VMEM, VMEM, VMEM, HBM, VMEM],
        out_specs=(VMEM,) * 3,
        scratch_shapes=[
            pltpu.VMEM((rows // groups, groups * ROPE), jnp.float32),
            pltpu.VMEM((slots, pages.shape[0], heads, width), jnp.float32),
            pltpu.VMEM((slots, heads, width), jnp.float32),
            pltpu.VMEM((slots, heads, width), jnp.float32),
            pltpu.VMEM((rows, latent), jnp.float32),
            pltpu.SemaphoreType.DMA,
            pltpu.SemaphoreType.DMA,
        ],
        input_output_aliases={5: 0},
        compiler_params=pltpu.CompilerParams(vmem_limit_bytes=40 * 2**20),
        name="attend",
    )(tiles, owner, count, queries.reshape(rows, channels), pool, pages)
    return keep, send


def tail_of(top, total, dtype):
    lane = lax.broadcasted_iota(jnp.int32, (*top.shape[:-1], LANES), top.ndim - 1)
    tail = jnp.zeros(lane.shape, jnp.float32)
    terms = []
    for value in (top, total):
        for _ in range(1 if dtype == jnp.float32 else 3):
            term = value.astype(dtype).astype(jnp.float32)
            terms.append(term)
            value = value - term
    for i, term in enumerate(terms):
        tail = jnp.where(lane == i, term, tail)
    return tail.astype(dtype)


def split_tail(tail):
    wide = tail.astype(jnp.float32)
    count = 1 if tail.dtype == jnp.float32 else 3
    parts = [wide[..., i : i + 1] for i in range(2 * count)]
    return sum(parts[1:count], parts[0]), sum(parts[count + 1 :], parts[count])


def combine(refs, rows):
    last = refs[0].shape[0] - 1
    tops, totals = zip(*[split_tail(ref[last, rows]) for ref in refs])
    top = functools.reduce(jnp.maximum, tops)
    scales = [jnp.exp(x - top) for x in tops]
    numer = [
        sum(ref[i, rows].astype(jnp.float32) * scale for ref, scale in zip(refs, scales))
        for i in range(last)
    ]
    return numer, top, sum(total * scale for total, scale in zip(totals, scales))


def merge_kernel(mine_ref, theirs_ref, *out_refs):
    cut = out_refs[0].shape[1]
    for part, ref in reversed(list(enumerate(out_refs))):
        numer, top, total = combine((mine_ref, theirs_ref), pl.ds(part * cut, cut))
        for i, value in enumerate(numer):
            ref[i] = value.astype(ref.dtype)
        ref[len(numer)] = tail_of(top, total, ref.dtype)


def finish_kernel(*refs):
    *refs, out_ref = refs
    numer, _, total = combine(refs, slice(None))
    for i, value in enumerate(numer):
        out_ref[:, i * LANES : (i + 1) * LANES] = (value / total).astype(out_ref.dtype)


def merge(mine, theirs, wires):
    tiles, rows, _ = mine.shape
    part = (tiles, rows // (1 + len(wires)), LANES)
    return pl.pallas_call(
        merge_kernel,
        out_shape=tuple(pltpu.VMEM(part, dtype) for dtype in (jnp.float32, *wires)),
        in_specs=[VMEM, VMEM],
        out_specs=(VMEM,) * (1 + len(wires)),
        compiler_params=pltpu.CompilerParams(vmem_limit_bytes=2**21),
        name=f"merge{rows}",
    )(mine, theirs)


def finish(*parts):
    tiles, rows, _ = parts[0].shape
    return pl.pallas_call(
        finish_kernel,
        out_shape=jax.ShapeDtypeStruct((rows, (tiles - 1) * LANES), jnp.bfloat16),
        in_specs=[VMEM] * len(parts),
        out_specs=VMEM,
        compiler_params=pltpu.CompilerParams(vmem_limit_bytes=2**20),
        name="finish",
    )(*parts)


def local(queries, kv_pages, page_table, lengths, selected):
    pages_dev, tokens = kv_pages.shape[:2]
    devices = lax.axis_size("head")
    strides = [1 << b for b in reversed(range(devices.bit_length() - 1))]
    width = LANES if pages_dev % LANES == 0 else pages_dev
    slots = pages_dev // width

    def swap(x, offset):
        return lax.ppermute(x, "head", [(i, i ^ offset) for i in range(devices)])

    pool = in_hbm(kv_pages.transpose(1, 2, 0))
    asked = queries.transpose(1, 0, 2)
    far = [strides[0], strides[1], strides[0] ^ strides[1]]
    arriving = [swap(asked, offset) for offset in far]
    owner, count, tiles, own = plan(lengths, page_table, selected, asked, slots, width, tokens)
    gathered = jnp.concatenate([own, *arriving], axis=0)
    ahead = tokens * 5 // 8
    for i, stride in enumerate(strides[2:]):
        gathered = lax.optimization_barrier(gathered)
        arriving = swap(gathered, stride)
        if i == 0:
            pages = fetch(tiles, pool, width, ahead)
            gathered, pages = lax.optimization_barrier((gathered, pages))
        gathered = jnp.concatenate([gathered, arriving], axis=0)
    keep, send = attend(gathered.transpose(1, 0, 2), pages, pool, (owner, count, tiles), ahead)
    theirs = swap(send, strides[-1])
    for stride in reversed(strides[3:-1]):
        keep, send = merge(keep, theirs, [jnp.bfloat16])
        theirs = swap(send, stride)
    keep, send = merge(keep, theirs, [jnp.bfloat16])
    keep, *sends = merge(keep, swap(send, strides[2]), WIRES)
    got = [swap(x, offset) for x, offset in reversed(list(zip(sends, far)))]
    return finish(keep, *got)[:, None, :]


def solution(mesh):
    return jax.shard_map(
        local,
        mesh=mesh,
        in_specs=(
            P("grp", "head", None),
            P(("grp", "head"), None, None),
            P("grp", None),
            P("grp"),
            P("grp", None),
        ),
        out_specs=P("grp", "head", None),
        check_vma=False,
    )
```
